128 devices in a mesh: tensor: 4 (over x), feat: 32 (over y, z, core).
Axes of the slice: x: 4, y: 4, z: 4, core: 2. Of those that a mesh axis runs over, the one named last changes fastest.
Arguments:
- feat_ids: int32 [512, 32], P('feat'), may hold values from 0 to 131071, as said below
- feat_acts: float32 [512, 32], P('feat'), may hold values from 0.1 to 3
- target_ids: int32 [1024], replicated, may hold values from 0 to 131071
- target_token_positions: int32 [1024], replicated, may hold values from 0 to 511
- encoder: bfloat16 [131072, 4608], P('feat', 'tensor'), may hold values from -0.59765625 to 0.59765625
- decoder: bfloat16 [131072, 4608], P('feat', 'tensor'), may hold values from -0.59765625 to 0.59765625
- queries: bfloat16 [512, 2048], P('feat', 'tensor'), may hold values from -6 to 6
- keys: bfloat16 [512, 1024], P('feat', 'tensor'), may hold values from -6 to 6
- w_out: bfloat16 [2048, 4608], P(None, 'tensor'), may hold values from -1.1953125 to 1.1953125
- w_value: bfloat16 [4608, 1024], P('tensor'), may hold values from -1.1953125 to 1.1953125
- ln_gain: float32 [4608], P('tensor'), may hold values from 0.3 to 3
- norm_scale: float32 [512], P('feat'), may hold values from 0.3 to 3
Outputs:
- edges: float32 [512, 32, 1024], P('feat', None, 'tensor')
The draws below stay inside these ranges and needn't reach their ends.
Inputs may be any that keep to these rules, and one draw needn't show every extreme that they name: `feat_ids`: split the ids into aligned blocks of 512 entries (the tokens of one device, in order) and the ids into feature blocks of 4096 (id // 4096): no feature block holds more than 64 entries of one token block, and one feature block holds exactly 64 entries of every token block.
All inputs are finite; a program needn't handle non-finite values.
Results may differ from the reference program's by a relative error of at most 0.0085.
Values may be sent and summed in bfloat16 or wider, within the bound.
A program may use at most 128 MiB of HBM per device.

```python
import math
import jax
import jax.numpy as jnp
from jax import lax

D = 4608
HD = 128
H = 16
KVH = 8
FEAT_DEV = 4096
TOK_DEV = 16
ACTIVE = 32
TARGETS = 1024
TOKENS = 512
FEATS = 131072
CAP = 64
N_FEAT = 32


def draw_feat_ids(key, part):
    slot_count = TOK_DEV * ACTIVE
    hot_key, block_key, row_key = jax.random.split(jax.random.fold_in(key, 11), 3)
    hot_owner = jax.random.randint(hot_key, (), 0, N_FEAT, dtype=jnp.int32)
    others = (hot_owner + 1 + jnp.arange((N_FEAT - 1) * CAP, dtype=jnp.int32) // CAP) % N_FEAT

    def one_block(block_random_key):
        pick_key, order_key = jax.random.split(block_random_key)
        picked = jax.random.permutation(pick_key, others)[:slot_count - CAP]
        owners = jnp.concatenate([jnp.full((CAP,), hot_owner, dtype=jnp.int32), picked])
        return jax.random.permutation(order_key, owners)
    owners = jax.vmap(one_block)(jax.random.split(block_key, N_FEAT))
    row_within = jax.random.randint(row_key, (N_FEAT, slot_count), 0, FEAT_DEV, dtype=jnp.int32)
    return (owners * FEAT_DEV + row_within).reshape(TOKENS, ACTIVE).astype(jnp.int32)


def plant(result, key, least, high):
    dims = result.shape
    spot = [jax.random.randint(jax.random.fold_in(key, axis), (), 0, dims[axis]) for axis in range(len(dims))]
    result = result.at[tuple(spot)].set(least)
    longest = dims.index(max(dims))
    spot[longest] = (spot[longest] + 1) % dims[longest]
    return result.at[tuple(spot)].set(high)


def block_levels(rng, extent, cuts, smallest, high):
    gain = 1.0
    for position, blocks in cuts:
        heights = jax.random.uniform(jax.random.fold_in(jax.random.fold_in(rng, 6), position), (blocks,), jnp.float32, smallest / len(cuts), high / len(cuts))
        gain = gain * jnp.repeat(jnp.exp(heights), extent[position] // blocks).reshape((-1,) + (1,) * (len(extent) - 1 - position))
    return gain


def scatter_about(key, shape, deviation, most, cuts=(), held_as=jnp.bfloat16):
    array = jax.random.normal(key, shape, jnp.float32) * deviation
    if len(cuts) > 0:
        array = block_levels(key, shape, cuts, -0.22, 0.18) * array
    return jnp.clip(array, min=-most, max=most).astype(held_as)


def setup_inputs(seed: int = 0) -> dict:
    key_of = jax.random.split(jax.random.key(seed), 13)
    return {
        "feat_ids": draw_feat_ids(jax.random.fold_in(key_of[12], 71), 0),
        "feat_acts": jnp.clip(jnp.exp(math.log(3.0) - 3.4011974 * jax.random.uniform(key_of[1], (TOKENS, ACTIVE), jnp.float32) ** block_levels(key_of[1], (TOKENS, ACTIVE), ((0, 32),), -0.2, 0.2)), 0.1, 3.0),
        "target_ids": plant(jax.random.randint(key_of[2], (TARGETS,), 0, FEATS), jax.random.fold_in(key_of[2], 1), 0, FEATS - 1).astype(jnp.int32),
        "target_token_positions": plant(jax.random.randint(key_of[3], (TARGETS,), 0, TOKENS), jax.random.fold_in(key_of[3], 1), 0, TOKENS - 1).astype(jnp.int32),
        "encoder": scatter_about(key_of[4], (FEATS, D), 0.1, 0.59765625, ((0, 32), (1, 4))),
        "decoder": scatter_about(key_of[5], (FEATS, D), 0.1, 0.59765625, ((0, 32), (1, 4))),
        "queries": scatter_about(key_of[6], (TOKENS, H * HD), 1.0, 6.0, ((0, 32), (1, 4))),
        "keys": scatter_about(key_of[7], (TOKENS, KVH * HD), 1.0, 6.0, ((0, 32), (1, 4))),
        "w_out": scatter_about(key_of[8], (H * HD, D), 0.2, 1.1953125, ((1, 4),)),
        "w_value": scatter_about(key_of[9], (D, KVH * HD), 0.2, 1.1953125, ((0, 4),)),
        "ln_gain": jnp.clip(jnp.exp(math.log(3.0) - 2.3025851 * jax.random.uniform(key_of[10], (D,), jnp.float32) ** block_levels(key_of[10], (D,), ((0, 4),), -0.2, 0.2)), 0.3, 3.0),
        "norm_scale": jnp.clip(jnp.exp(math.log(3.0) - 2.3025851 * jax.random.uniform(key_of[11], (TOKENS,), jnp.float32) ** block_levels(key_of[11], (TOKENS,), ((0, 32),), -0.2, 0.2)), 0.3, 3.0),
    }


softcap_value = 50.0
query_scale = 144.0 ** -0.5
largest_precision = lax.Precision.HIGHEST


def reference(feat_ids, feat_acts, target_ids, target_token_positions, encoder, decoder, queries, keys, w_out, w_value, ln_gain, norm_scale):
    groups = H // KVH
    seed_row_block = encoder[target_ids]
    query_rows = queries[target_token_positions].astype(jnp.float32).reshape(TARGETS, KVH, groups, HD)
    key_heads = keys.astype(jnp.float32).reshape(TOKENS, KVH, HD)
    scores = jnp.einsum('bkge,tke->bkgt', query_rows, key_heads, precision=largest_precision) * query_scale
    capped = softcap_value * jnp.tanh(scores / softcap_value)
    positions = jnp.arange(TOKENS, dtype=jnp.int32)
    causal = positions[None, :] <= target_token_positions[:, None]
    weights = jnp.where(causal[:, None, None, :], jnp.exp(capped), jnp.float32(0.0))
    pattern = weights / jnp.sum(weights, axis=3, keepdims=True)
    back_full = jnp.dot(seed_row_block.astype(jnp.float32), w_out.astype(jnp.float32).T, precision=largest_precision)
    back_heads = lax.optimization_barrier(back_full.astype(jnp.bfloat16)).astype(jnp.float32)
    back_heads = back_heads.reshape(TARGETS, KVH, groups, HD)
    decoder_target_rows = decoder[feat_ids[target_token_positions]].astype(jnp.float32)
    direct_attribution = jnp.einsum('gnj,gj->gn', decoder_target_rows, seed_row_block.astype(jnp.float32), precision=largest_precision)
    value_table = w_value.astype(jnp.float32)
    block_size = math.gcd(TOKENS, 16)
    blocks = TOKENS // block_size
    pattern_blocks = pattern.reshape(TARGETS, KVH, groups, blocks, block_size).transpose(3, 0, 1, 2, 4)

    def one_block(inputs):
        ids_block, acts_block, scale_block, pattern_block, pos_block = inputs
        dec_rows = decoder[ids_block].astype(jnp.float32)
        gained = lax.optimization_barrier((dec_rows * ln_gain).astype(jnp.bfloat16)).astype(jnp.float32)
        projected = jnp.dot(gained.reshape(-1, D), value_table, precision=largest_precision)
        projected = lax.optimization_barrier(projected.astype(jnp.bfloat16)).astype(jnp.float32)
        projected = projected.reshape(block_size, ACTIVE, KVH * HD)
        value_grad = jnp.einsum('bkgt,bkge->tbke', pattern_block, back_heads, precision=largest_precision)
        value_grad = lax.optimization_barrier(value_grad.astype(jnp.bfloat16)).astype(jnp.float32)
        value_grad = value_grad.reshape(block_size, TARGETS, KVH * HD)
        attention = jnp.einsum('tkj,tbj->tkb', projected, value_grad, precision=largest_precision)
        at_target = pos_block[:, None] == target_token_positions[None, :]
        direct = jnp.where(at_target[:, None, :], direct_attribution.T[None, :, :], jnp.float32(0.0))
        return acts_block[:, :, None] * (direct + scale_block[:, None, None] * attention)

    edges = lax.map(one_block, (feat_ids.reshape(blocks, block_size, ACTIVE),
                                feat_acts.reshape(blocks, block_size, ACTIVE),
                                norm_scale.reshape(blocks, block_size),
                                pattern_blocks,
                                positions.reshape(blocks, block_size)))
    return edges.reshape(TOKENS, ACTIVE, TARGETS)
```

```python
import jax
import jax.numpy as jnp
from jax import lax
from jax.experimental import pallas as pl
from jax.experimental.pallas import tpu as pltpu
from jax.sharding import PartitionSpec as P

HD = 128
H = 16
KVH = 8
NX = 4
NF = 32
MESH = pl.DeviceIdType.MESH
F32 = jnp.float32
BF16 = jnp.bfloat16

softcap_value = 50.0
query_scale = 144.0 ** (-0.5)

VM = pl.BlockSpec(memory_space=pltpu.VMEM)
ANY = pl.BlockSpec(memory_space=pl.ANY)


def nt_dot(a, b):
    return lax.dot_general(a, b, (((1,), (1,)), ((), ())), preferred_element_type=F32)


def nn_dot(a, b):
    return lax.dot_general(a, b, (((1,), (0,)), ((), ())), preferred_element_type=F32)


def feat_id(y, z, c):
    return (y * 4 + z) * 2 + c


def barrier_with(devices):
    barrier = pltpu.get_barrier_semaphore()
    for dev in devices:
        pl.semaphore_signal(barrier, inc=1, device_id=dev, device_id_type=MESH)
    pl.semaphore_wait(barrier, len(devices))


class Copies:
    def __init__(self, send, recv):
        self.send, self.recv, self.all = send, recv, []

    def start(self, src, dst, dev):
        i = len(self.all)
        cp = pltpu.make_async_remote_copy(
            src_ref=src,
            dst_ref=dst,
            send_sem=self.send.at[i],
            recv_sem=self.recv.at[i],
            device_id=dev,
            device_id_type=MESH,
        )
        cp.start()
        self.all.append(cp)
        return cp

    def drain(self):
        for cp in self.all:
            cp.wait_send()


class RingSum:
    def __init__(self, copies, p, plus, minus, block, lo, hi, bufs):
        self.c, self.p, self.plus, self.minus = copies, p, plus, minus
        self.block, self.lo, self.hi = block, lo, hi
        self.lo_in, self.hi_in, self.m_in, self.p_in = bufs

    def at(self, d):
        return self.block((self.p + d) % 4)

    def step1(self):
        far = self.at(2)
        self.a = self.c.start(self.lo(far), self.lo_in, self.plus)
        self.b = self.c.start(self.hi(far), self.hi_in, self.minus)

    def step2(self):
        self.a.wait_recv()
        up = self.lo(self.at(1))
        up[...] = (up[...].astype(F32) + self.lo_in[...].astype(F32)).astype(BF16)
        self.a = self.c.start(self.at(1), self.m_in, self.plus)
        self.b.wait_recv()
        down = self.hi(self.at(3))
        down[...] = (down[...].astype(F32) + self.hi_in[...].astype(F32)).astype(BF16)
        self.b = self.c.start(self.at(3), self.p_in, self.minus)

    def result(self):
        self.a.wait_recv()
        self.b.wait_recv()
        return (
            self.at(0)[...].astype(F32) + self.m_in[...].astype(F32) + self.p_in[...].astype(F32)
        )


class RingGather:
    def __init__(self, copies, p, plus, minus, block, lo, hi):
        self.c, self.p, self.plus, self.minus = copies, p, plus, minus
        self.block, self.lo, self.hi = block, lo, hi

    def at(self, d):
        return self.block((self.p + d) % 4)

    def step1(self):
        own = self.at(0)
        self.a = self.c.start(own, own, self.plus)
        self.b = self.c.start(own, own, self.minus)

    def step2(self):
        self.a.wait_recv()
        left = self.lo(self.at(3))
        self.a = self.c.start(left, left, self.plus)
        self.b.wait_recv()
        right = self.hi(self.at(1))
        self.b = self.c.start(right, right, self.minus)

    def finish(self):
        self.a.wait_recv()
        self.b.wait_recv()


def ids_kernel(ids_ref, out_ref, send, recv):
    f = lax.axis_index("feat")
    barrier = pltpu.get_barrier_semaphore()

    def signal(d, carry):
        pl.semaphore_signal(
            barrier, inc=1, device_id={"feat": (f + d) % NF}, device_id_type=MESH
        )
        return carry

    lax.fori_loop(1, NF, signal, 0)
    out_ref[f] = ids_ref[...]
    pl.semaphore_wait(barrier, NF - 1)

    def copy(d):
        return pltpu.make_async_remote_copy(
            src_ref=ids_ref,
            dst_ref=out_ref.at[f],
            send_sem=send.at[d],
            recv_sem=recv.at[d],
            device_id={"feat": (f + d) % NF},
            device_id_type=MESH,
        )

    def start(d, carry):
        copy(d).start()
        return carry

    def wait(d, carry):
        copy(d).wait()
        return carry

    lax.fori_loop(1, NF, start, 0)
    lax.fori_loop(1, NF, wait, 0)


def gather_ids(ids):
    return pl.pallas_call(
        ids_kernel,
        out_shape=jax.ShapeDtypeStruct((NF, 4, 128), jnp.int32),
        in_specs=[VM],
        out_specs=VM,
        scratch_shapes=[pltpu.SemaphoreType.DMA((NF,)), pltpu.SemaphoreType.DMA((NF,))],
        compiler_params=pltpu.CompilerParams(collective_id=0, has_side_effects=True),
        name="ids",
    )(ids)


def seed_kernel(
    part, qk, wout_hbm, seeds, back, qk_all,
    r0, acc0,
    a_lo, a_hi, a_m, a_p, a_acc, a2_lo, a2_hi, a2_m, a2_p,
    b_lo, b_hi, b_m, b_p, b_acc, b2_lo, b2_hi, b2_m, b2_p,
    wout, bk, k_lo, k_hi, k_m, k_p,
    local, send, recv, qsend, qrecv,
):
    x = lax.axis_index("tensor")
    f = lax.axis_index("feat")
    c = f % 2
    z = (f // 2) % 4
    y = f // 8
    chip = f // 2
    wload = pltpu.make_async_copy(wout_hbm, wout, local.at[0])
    wload.start()
    at = lambda yy, zz, cc: {"feat": feat_id(yy, zz, cc)}
    partner = at(y, z, 1 - c)
    yp, ym = at((y + 1) % 4, z, c), at((y + 3) % 4, z, c)
    zp, zm = at(y, (z + 1) % 4, c), at(y, (z + 3) % 4, c)
    xp, xm = {"tensor": (x + 1) % 4}, {"tensor": (x + 3) % 4}

    barrier = pltpu.get_barrier_semaphore()

    def signal(d, carry):
        pl.semaphore_signal(
            barrier,
            inc=1,
            device_id={"feat": ((chip + d) % 16) * 2 + c},
            device_id_type=MESH,
        )
        return carry

    lax.fori_loop(1, 16, signal, 0)
    for dev in (partner, xp, xm):
        pl.semaphore_signal(barrier, inc=1, device_id=dev, device_id_type=MESH)
    qk_all[chip, c] = qk[...]
    pl.semaphore_wait(barrier, 18)

    cs = Copies(send, recv)
    core0 = cs.start(part.at[:, :, 1 - c], r0, partner)

    def qcopy(d):
        return pltpu.make_async_remote_copy(
            src_ref=qk,
            dst_ref=qk_all.at[chip, c],
            send_sem=qsend.at[d],
            recv_sem=qrecv.at[d],
            device_id={"feat": ((chip + d) % 16) * 2 + c},
            device_id_type=MESH,
        )

    core0.wait_recv()
    for yy in range(4):
        acc0[yy] = part[yy, :, c] + r0[yy]

    CA = pl.ds(0, 640)
    CB = pl.ds(640, 512)
    half0 = lambda r: r.at[pl.ds(0, 2)]
    half1 = lambda r: r.at[pl.ds(2, 2)]
    top = lambda r: r.at[pl.ds(0, 16)]
    bot = lambda r: r.at[pl.ds(16, 16)]
    ra = RingSum(cs, y, yp, ym, lambda q: acc0.at[q, :, :, CA], half0, half1, (a_lo, a_hi, a_m, a_p))
    rb = RingSum(cs, z, zp, zm, lambda q: acc0.at[:, q, :, CB], half0, half1, (b_lo, b_hi, b_m, b_p))
    ra.step1()
    rb.step1()
    ra.step2()
    rb.step2()
    a_acc[...] = ra.result().astype(BF16)
    ra2 = RingSum(cs, z, zp, zm, lambda q: a_acc.at[q], top, bot, (a2_lo, a2_hi, a2_m, a2_p))
    ra2.step1()
    b_acc[...] = rb.result().astype(BF16)
    rb2 = RingSum(cs, y, yp, ym, lambda q: b_acc.at[q], top, bot, (b2_lo, b2_hi, b2_m, b2_p))
    rb2.step1()
    ra2.step2()
    rb2.step2()
    seeds[y, z, c, :, 0:640] = ra2.result().astype(BF16)
    seeds[y, z, c, :, 640:1152] = rb2.result().astype(BF16)

    ga = RingGather(cs, z, zp, zm, lambda q: seeds.at[y, q, c, :, CA], top, bot)
    gb = RingGather(cs, y, yp, ym, lambda q: seeds.at[q, z, c, :, CB], top, bot)
    ga.step1()
    gb.step1()

    def qstart(d, carry):
        qcopy(d).start()
        return carry

    lax.fori_loop(1, 16, qstart, 0)

    wload.wait()
    mine = seeds[y, z, c]
    for n in range(4):
        bk[n] = nt_dot(mine, wout[pl.ds(n * 512, 512), :]).astype(BF16)
    rk = RingSum(cs, x, xp, xm, lambda q: bk.at[q], top, bot, (k_lo, k_hi, k_m, k_p))
    rk.step1()
    ga.step2()
    gb.step2()
    rk.step2()
    ga.finish()
    ga2 = RingGather(cs, y, yp, ym, lambda q: seeds.at[q, :, c, :, CA], half0, half1)
    ga2.step1()
    gb.finish()
    gb2 = RingGather(cs, z, zp, zm, lambda q: seeds.at[:, q, c, :, CB], half0, half1)
    gb2.step1()
    back[y, z, c] = rk.result().astype(BF16)
    KA = pl.ds(0, 256)
    KB = pl.ds(256, 256)
    ha = RingGather(cs, z, zp, zm, lambda q: back.at[y, q, c, :, KA], top, bot)
    hb = RingGather(cs, y, yp, ym, lambda q: back.at[q, z, c, :, KB], top, bot)
    ha.step1()
    hb.step1()

    def qwait(d, carry):
        qcopy(d).wait()
        return carry

    lax.fori_loop(1, 16, qwait, 0)
    qx = cs.start(qk_all.at[:, c], qk_all.at[:, c], partner)

    ga2.step2()
    gb2.step2()
    ha.step2()
    hb.step2()
    ha.finish()
    ha2 = RingGather(cs, y, yp, ym, lambda q: back.at[q, :, c, :, KA], half0, half1)
    ha2.step1()
    hb.finish()
    hb2 = RingGather(cs, z, zp, zm, lambda q: back.at[:, q, c, :, KB], half0, half1)
    hb2.step1()
    ga2.finish()
    gb2.finish()
    sx = cs.start(seeds.at[:, :, c], seeds.at[:, :, c], partner)
    ha2.step2()
    hb2.step2()
    ha2.finish()
    hb2.finish()
    bx = cs.start(back.at[:, :, c], back.at[:, :, c], partner)
    qx.wait_recv()
    sx.wait_recv()
    bx.wait_recv()
    cs.drain()


def seed_call(part, qk, w_out):
    ring = lambda lead: [
        pltpu.VMEM((2, 32, lead), BF16), pltpu.VMEM((2, 32, lead), BF16),
        pltpu.VMEM((4, 32, lead), BF16), pltpu.VMEM((4, 32, lead), BF16),
        pltpu.VMEM((4, 32, lead), BF16),
        pltpu.VMEM((16, lead), BF16), pltpu.VMEM((16, lead), BF16),
        pltpu.VMEM((32, lead), BF16), pltpu.VMEM((32, lead), BF16),
    ]
    return pl.pallas_call(
        seed_kernel,
        out_shape=(
            jax.ShapeDtypeStruct((4, 4, 2, 32, 1152), BF16),
            jax.ShapeDtypeStruct((4, 4, 2, 32, 512), BF16),
            jax.ShapeDtypeStruct((16, 2, 16, 768), BF16),
        ),
        in_specs=[VM, VM, ANY],
        out_specs=(VM, VM, VM),
        scratch_shapes=[
            pltpu.VMEM((4, 4, 32, 1152), BF16), pltpu.VMEM((4, 4, 32, 1152), BF16),
            *ring(640), *ring(512),
            pltpu.VMEM((2048, 1152), BF16), pltpu.VMEM((4, 32, 512), BF16),
            pltpu.VMEM((16, 512), BF16), pltpu.VMEM((16, 512), BF16),
            pltpu.VMEM((32, 512), BF16), pltpu.VMEM((32, 512), BF16),
            pltpu.SemaphoreType.DMA((1,)),
            pltpu.SemaphoreType.DMA((64,)), pltpu.SemaphoreType.DMA((64,)),
            pltpu.SemaphoreType.DMA((16,)), pltpu.SemaphoreType.DMA((16,)),
        ],
        compiler_params=pltpu.CompilerParams(collective_id=1, has_side_effects=True),
        name="seeds",
    )(part, qk, w_out)


def pattern_kernel(qk, pos, out, e_ref):
    f = lax.axis_index("feat")
    tokens = qk.shape[0]
    t = lax.broadcasted_iota(jnp.int32, (tokens, tokens), 0)
    p = lax.broadcasted_iota(jnp.int32, (tokens, tokens), 1)
    causal = t <= p
    pick = (
        lax.broadcasted_iota(jnp.int32, (tokens, pos.shape[1]), 0) == pos[...]
    ).astype(BF16)
    for h in range(4):
        kv = h // 2
        scores = nt_dot(
            qk[:, 512 + kv * HD : 512 + (kv + 1) * HD], qk[:, h * HD : (h + 1) * HD]
        ) * query_scale
        capped = softcap_value * jnp.tanh(scores / softcap_value)
        e = jnp.where(causal, jnp.exp(capped), 0.0)
        e_ref[...] = e
        total = jnp.sum(e, axis=0, keepdims=True)
        own = e_ref[pl.ds(pl.multiple_of(f * 16, 16), 16), :] / total
        head = own.astype(BF16)
        rest = (own - head.astype(F32)).astype(BF16)
        out[h] = nn_dot(head, pick) + nn_dot(rest, pick)


def pattern_call(qk, pos):
    return pl.pallas_call(
        pattern_kernel,
        out_shape=jax.ShapeDtypeStruct((4, 16, 1024), F32),
        in_specs=[VM, VM],
        out_specs=VM,
        scratch_shapes=[pltpu.VMEM((512, 512), F32)],
        name="pattern",
    )(qk, pos)


def tail_kernel(
    recv_hbm, sel, gain, wv, seeds, back, pat, pos, acts, scale, out,
    rows, fetched, projp, proj, direct, edge,
    p_lo, p_hi, p_m, p_p, e_lo, e_hi, e_m, e_p, local, send, recv,
):
    x = lax.axis_index("tensor")
    f = lax.axis_index("feat")
    xp, xm = {"tensor": (x + 1) % 4}, {"tensor": (x + 3) % 4}
    load = pltpu.make_async_copy(recv_hbm, rows, local.at[0])
    load.start()
    barrier_with([xp, xm])
    cs = Copies(send, recv)
    load.wait()

    slots = rows.shape[0]

    def select(i, carry):
        r = pl.ds(pl.multiple_of(i * 128, 128), 128)
        onehot = (
            lax.broadcasted_iota(jnp.int32, (128, slots), 1) == sel[r, :]
        ).astype(BF16)
        got = nn_dot(onehot, rows[...]).astype(BF16)
        fetched[r, :] = got
        gained = (got.astype(F32) * gain[...]).astype(BF16)
        for n in range(4):
            projp[n, r, :] = nn_dot(gained, wv[:, n * 256 : (n + 1) * 256]).astype(BF16)
        return carry

    lax.fori_loop(0, 4, select, 0)
    half0 = lambda r: r.at[pl.ds(0, 256)]
    half1 = lambda r: r.at[pl.ds(256, 256)]
    rp = RingSum(cs, x, xp, xm, lambda q: projp.at[q], half0, half1, (p_lo, p_hi, p_m, p_p))
    rp.step1()

    token = f * 16 + lax.broadcasted_iota(jnp.int32, (512, 256), 0) // 32

    def direct_block(n):
        cols = slice(n * 256, (n + 1) * 256)
        d = nt_dot(fetched[...], seeds[cols, :])
        direct[n] = jnp.where(token == pos[:, cols], d, 0.0)

    direct_block(0)
    direct_block(1)
    rp.step2()
    direct_block(2)
    direct_block(3)
    proj[...] = rp.result().astype(BF16)

    def edge_block(d):
        n = (x + d) % 4
        cols = pl.ds(pl.multiple_of(n * 256, 256), 256)
        for g in range(4):
            r = pl.ds(g * 128, 128)
            acc = jnp.zeros((128, 256), F32)
            for h in range(4):
                kv = h // 2
                mm = nt_dot(
                    proj[r, kv * HD : (kv + 1) * HD], back[cols, h * HD : (h + 1) * HD]
                )
                w = pat[h, pl.ds(g * 4, 4), cols]
                acc = acc + (mm.reshape(4, 32, 256) * w[:, None, :]).reshape(128, 256)
            edge[n, r, :] = (acts[r, :] * (direct[n, r, :] + scale[r, :] * acc)).astype(BF16)

    re = RingSum(cs, x, xp, xm, lambda q: edge.at[q], half0, half1, (e_lo, e_hi, e_m, e_p))
    edge_block(2)
    re.step1()
    edge_block(1)
    edge_block(3)
    re.step2()
    edge_block(0)
    out[...] = re.result()
    cs.drain()


def tail_call(recv, sel, gain, wv, seeds, back, pat, pos, acts, scale):
    half = pltpu.VMEM((256, 256), BF16)
    full = pltpu.VMEM((512, 256), BF16)
    return pl.pallas_call(
        tail_kernel,
        out_shape=jax.ShapeDtypeStruct((512, 256), F32),
        in_specs=[ANY] + [VM] * 9,
        out_specs=VM,
        scratch_shapes=[
            pltpu.VMEM((2048, 1152), BF16), pltpu.VMEM((512, 1152), BF16),
            pltpu.VMEM((4, 512, 256), BF16), full,
            pltpu.VMEM((4, 512, 256), F32), pltpu.VMEM((4, 512, 256), BF16),
            half, half, full, full, half, half, full, full,
            pltpu.SemaphoreType.DMA((1,)),
            pltpu.SemaphoreType.DMA((8,)), pltpu.SemaphoreType.DMA((8,)),
        ],
        compiler_params=pltpu.CompilerParams(collective_id=2, has_side_effects=True),
        name="tail",
    )(recv, sel, gain, wv, seeds, back, pat, pos, acts, scale)


def per_device(
    feat_ids, feat_acts, target_ids, target_token_positions, encoder, decoder,
    queries, keys, w_out, w_value, ln_gain, norm_scale,
):
    f = lax.axis_index("feat")
    feat_dev = encoder.shape[0]
    targets = target_ids.shape[0]
    cap = 64
    ids_all = gather_ids(feat_ids.reshape(4, 128)).reshape(NF, 512)
    owner_all = ids_all // feat_dev
    local_all = ids_all - owner_all * feat_dev
    mine = owner_all == f
    upper = (
        lax.broadcasted_iota(jnp.int32, (512, 512), 0)
        < lax.broadcasted_iota(jnp.int32, (512, 512), 1)
    )
    rank = jnp.dot(mine.astype(BF16), upper.astype(BF16), preferred_element_type=F32)
    key = jnp.where(mine, rank.astype(jnp.int32), -1)
    slots = jnp.arange(cap, dtype=jnp.int32)
    wanted = jnp.sum(
        jnp.where(key[:, None, :] == slots[None, :, None], local_all[:, None, :], 0), axis=2
    )
    found = decoder[wanted.reshape(-1)].reshape(NF, cap, -1)
    returned = lax.all_to_all(found, "feat", split_axis=0, concat_axis=0, tiled=True)

    ids = feat_ids.reshape(512)
    own = ids // feat_dev
    same = (own[:, None] == own[None, :]) & upper.T
    slot = jnp.sum(same.astype(jnp.int32), axis=1)
    sel = (own * cap + slot)[:, None]

    target_owner = target_ids // feat_dev
    target_row = target_ids - target_owner * feat_dev
    is_owner = (target_owner == f)[:, None]
    part = jnp.where(is_owner, encoder[target_row], jnp.zeros((), BF16))
    qk = jnp.concatenate([queries, keys], axis=1)
    seeds, back, qk_all = seed_call(part.reshape(4, 4, 2, 32, -1), qk, w_out)
    pos = target_token_positions[None, :]
    pat = pattern_call(qk_all.reshape(512, 768), pos)
    out = tail_call(
        returned.reshape(NF * cap, -1), sel, ln_gain[None, :], w_value,
        seeds.reshape(targets, -1), back.reshape(targets, -1), pat, pos,
        feat_acts.reshape(512, 1), jnp.repeat(norm_scale, 32)[:, None],
    )
    return out.reshape(16, 32, 256)


def solution(mesh):
    in_specs = (
        P("feat", None),
        P("feat", None),
        P(),
        P(),
        P("feat", "tensor"),
        P("feat", "tensor"),
        P("feat", "tensor"),
        P("feat", "tensor"),
        P(None, "tensor"),
        P("tensor", None),
        P("tensor"),
        P("feat"),
    )
    out_specs = P("feat", None, "tensor")
    return jax.shard_map(
        per_device, mesh=mesh, in_specs=in_specs, out_specs=out_specs, check_vma=False
    )
```
